32 devices in a mesh: rep: 2 (over y), dp: 4 (over x, core), tensor: 4 (over z).
Axes of the slice: x: 2, y: 2, z: 4, core: 2. Of those that a mesh axis runs over, the one named last changes fastest.
Arguments:
- activations: bfloat16 [12288, 8192], P(('rep', 'dp'), 'tensor'), parts along dimension 0, may hold values from -6 to 6
- output_gradient: bfloat16 [12288, 2048], P(('rep', 'dp'), 'tensor'), parts along dimension 0, may hold values from -6 to 6
- row_tenant: int32 [12288, 1], P(('rep', 'dp')), parts along dimension 0, may hold values from 0 to 15; in each aligned block of 1536 rows (0 to 1535, 1536 to 3071, ...) at most 192 rows name the same one
- group_row_count: int32 [8], P(('rep', 'dp')), parts along dimension 0, may hold values from 384 to 1536
- tenant_storage_entry: int32 [16], replicated, may hold values from 0 to 15, each once
- key_value_weight: bfloat16 [8192, 2048], P('tensor'), may hold values from -0.125 to 0.125
- adapter_down_maps: bfloat16 [16, 8192, 64], P('dp', 'tensor'), may hold values from -0.23925781 to 0.23925781
- adapter_up_maps: bfloat16 [16, 64, 2048], P('dp', None, 'tensor'), may hold values from -0.125 to 0.125
- down_row_factor: float32 [16, 8192], P('dp', 'tensor'), may hold values from 2 to 60
- down_column_factor: float32 [16, 64], P('dp'), may hold values from 2 to 60
- up_row_factor: float32 [16, 64], P('dp'), may hold values from 0.02 to 0.6
- up_column_factor: float32 [16, 2048], P('dp', 'tensor'), may hold values from 20 to 600
Outputs:
- input_grad: bfloat16 [12288, 8192], P(('rep', 'dp'), 'tensor'), parts along dimension 0
- down_rows: float32 [32, 8192], P(('rep', 'dp'), 'tensor'), parts along dimension 0
- down_cols: float32 [32, 64], P(('rep', 'dp')), parts along dimension 0
- up_rows: float32 [32, 64], P(('rep', 'dp')), parts along dimension 0
- up_cols: float32 [32, 2048], P(('rep', 'dp'), 'tensor'), parts along dimension 0
- down_update: float32 [32, 8192, 64], P(('rep', 'dp'), 'tensor'), parts along dimension 0
- up_update: float32 [32, 64, 2048], P(('rep', 'dp'), None, 'tensor'), parts along dimension 0
The draws below stay inside these ranges and needn't reach their ends.
There are 2 independent parts, one for each index of `rep`. The reference program is written for one: setup_inputs(seed, part) draws one part's arguments, and reference() takes and returns one part's arrays. A program takes and returns all parts, laid end to end along the dimension named above; an argument that names none is the same for every part. Nothing has to cross between parts.
Inputs may be any that keep to these rules, and one draw needn't show every extreme that they name: `row_tenant`: within the rows of one group (aligned blocks of 1536 rows, padding rows included) no tenant is named by more than 192 rows, a bound that some block reaches. Row 1536 g + i is live for i < group_row_count[g]; the other rows of the group are padding. A permutation: tenant t's adapters and factors are stored at entry tenant_storage_entry[t] of the adapter and factor arrays.
All inputs are finite; a program needn't handle non-finite values.
Results may differ from the reference program's by a relative error of at most 0.0029.
Values may be sent and summed in bfloat16 or wider, within the bound.
No kernel may reach another device: no remote copies, remote signals or barrier semaphores. Data moves between devices by JAX's collectives and lax.ppermute only.
A program may use at most 128 MiB of HBM per device.

```python
import math
import jax
import jax.numpy as jnp
import numpy as np
from jax import lax

MODEL_WIDTH = 8192
ADAPTER_RANK = 64
TOK = 1536
KEY_VALUE_WIDTH = 2048
TOKENS = 6144
TENANT_TOTAL = 16
TENANT_ROW_LIMIT = 192
N_DP = 4


def plant(drawn, own_key, low, top_value):
    longest = drawn.shape.index(max(drawn.shape))
    spots = []
    for shift in (0, 1):
        where = [jax.random.randint(jax.random.fold_in(own_key, axis), (), 0, length) for axis, length in enumerate(drawn.shape)]
        where[longest] = (where[longest] + shift) % drawn.shape[longest]
        spots.append(tuple(where))
    return drawn.at[spots[0]].set(low).at[spots[1]].set(top_value)


def block_levels(stream_key, extent, split, smallest, high):
    def one(dim, parts):
        draws = jax.random.uniform(jax.random.fold_in(jax.random.fold_in(stream_key, 6), dim), (parts,), jnp.float32, smallest / len(split), high / len(split))
        return jnp.repeat(jnp.exp(draws), extent[dim] // parts).reshape((-1,) + (1,) * (len(extent) - dim - 1))

    loudness = one(*split[0])
    for cut in split[1:]:
        loudness = loudness * one(*cut)
    return loudness


def shared_out(own_key, own, number, rows, count, top, most, lean):
    ranking = jax.random.permutation(own_key, count)
    heavy_load, ordinary = load_shares(count, rows * top, most, lean, True), load_shares(count, rows * top, most, lean, False)
    places = jnp.arange(count)

    def named(tallies, turn):
        used = int((tallies > 0).sum())
        fixed = max(1, used // 4)
        moved = fixed + (places - fixed + turn * (used - fixed)) % max(1, count - fixed)
        return jnp.zeros((count,), jnp.int32).at[ranking[jnp.where(places < fixed, places, moved)]].set(jnp.asarray(tallies, jnp.int32))

    tallies = jnp.where(number % 4 == 0, named(heavy_load, number // 4), named(ordinary, number - number // 4 - 1))
    mixed = jax.random.permutation(jax.random.fold_in(own, 3), count)
    source_of, taker = mixed[0:count // 2 * 2:2], mixed[1:count // 2 * 2:2]
    margin = jnp.minimum(tallies[source_of] - 1, most - tallies[taker]) // 2
    margin = jnp.where((source_of == ranking[0]) | (taker == ranking[0]) | (tallies[taker] == 0), 0, jnp.maximum(margin, 0))
    moved = jax.random.randint(jax.random.fold_in(own, 4), (count // 2,), 0, 1 << 20) % (margin + 1)
    tallies = tallies.at[source_of].add(-moved).at[taker].add(moved)
    members = jnp.searchsorted(jnp.cumsum(tallies), jnp.arange(rows * top), side="right").astype(jnp.int32)
    table = members.reshape(top, rows).T
    table = table[jax.random.permutation(jax.random.fold_in(own, 1), rows)]
    turn = jax.random.randint(jax.random.fold_in(own, 2), (rows, 1), 0, top)
    return jnp.take_along_axis(table, (jnp.arange(top)[None, :] + turn) % top, axis=1)


def load_shares(number_of, total, limit, skew, full):
    portions = [(1 << 20) // math.isqrt(rank ** skew) + 1 for rank in range(1, number_of + 1)]
    largest = limit if full else min(limit, max(-(-total // number_of), total * portions[0] // sum(portions)))
    least = 1 if total - largest >= number_of - 1 else 0
    given, spare = [largest] + [least] * (number_of - 1), total - largest - least * (number_of - 1)
    while spare > 0:
        free = [i for i in range(1, number_of) if given[i] < largest] or [i for i in range(1, number_of) if given[i] < limit]
        whole, remaining = sum([portions[i] for i in free]), spare
        for i in free:
            more = min(limit - given[i], max(1, remaining * portions[i] // whole), spare)
            given[i] = given[i] + more
            spare = spare - more
    return np.array(given)


def bell_draw(rng, dims, spread, bound, shards=(), kind=jnp.bfloat16):
    drawn = jax.random.normal(rng, dims, jnp.float32) * spread
    if len(shards) > 0:
        drawn = block_levels(rng, dims, shards, -0.22, 0.18) * drawn
    return jnp.clip(drawn, min=-bound, max=bound).astype(kind)


def setup_inputs(seed: int = 0, part: int = 0) -> dict:
    splits = jax.random.split(jax.random.key(seed), 13)
    part_keys = jax.random.split(jax.random.fold_in(splits[12], part), 13)
    activations = bell_draw(part_keys[0], (TOKENS, MODEL_WIDTH), 1.0, 6.0, ((0, 4), (1, 4)))
    output_gradient = bell_draw(part_keys[1], (TOKENS, KEY_VALUE_WIDTH), 1.0, 6.0, ((0, 4), (1, 4)))
    row_tenant_keys = jax.random.split(jax.random.fold_in(part_keys[2], 1), TOKENS // TOK)
    row_tenant_turns = jax.random.permutation(jax.random.fold_in(part_keys[2], 3), TOKENS // TOK)
    row_tenant = jax.vmap(lambda own, number: shared_out(jax.random.fold_in(part_keys[2], 2), own, number, TOK, TENANT_TOTAL, 1, TENANT_ROW_LIMIT, 2))(row_tenant_keys, row_tenant_turns).reshape((TOKENS, 1))
    group_row_count = plant(jax.random.randint(part_keys[3], (N_DP,), TOK // 4, TOK + 1), jax.random.fold_in(part_keys[3], 1), TOK // 4, TOK).astype(jnp.int32)
    tenant_storage_entry = jax.random.permutation(splits[4], TENANT_TOTAL).astype(jnp.int32)
    key_value_weight = bell_draw(splits[5], (MODEL_WIDTH, KEY_VALUE_WIDTH), KEY_VALUE_WIDTH ** -0.5, 0.125, ((0, 4),))
    adapter_down_maps = bell_draw(splits[6], (TENANT_TOTAL, MODEL_WIDTH, ADAPTER_RANK), 0.04, 0.23925781, ((0, 4), (1, 4)))
    adapter_up_maps = bell_draw(splits[7], (TENANT_TOTAL, ADAPTER_RANK, KEY_VALUE_WIDTH), KEY_VALUE_WIDTH ** -0.5, 0.125, ((0, 4), (2, 4)))
    down_row_factor = jnp.clip(jnp.exp(math.log(60.0) - 3.4011974 * jax.random.uniform(splits[8], (TENANT_TOTAL, MODEL_WIDTH), jnp.float32) ** block_levels(splits[8], (TENANT_TOTAL, MODEL_WIDTH), ((0, 4), (1, 4)), -0.2, 0.2)), 2.0, 60.0)
    down_column_factor = jnp.clip(jnp.exp(math.log(60.0) - 3.4011974 * jax.random.uniform(splits[9], (TENANT_TOTAL, ADAPTER_RANK), jnp.float32) ** block_levels(splits[9], (TENANT_TOTAL, ADAPTER_RANK), ((0, 4),), -0.2, 0.2)), 2.0, 60.0)
    up_row_factor = jnp.clip(jnp.exp(math.log(0.6) - 3.4011974 * jax.random.uniform(splits[10], (TENANT_TOTAL, ADAPTER_RANK), jnp.float32) ** block_levels(splits[10], (TENANT_TOTAL, ADAPTER_RANK), ((0, 4),), -0.2, 0.2)), 0.02, 0.6)
    up_column_factor = jnp.clip(jnp.exp(math.log(600.0) - 3.4011974 * jax.random.uniform(splits[11], (TENANT_TOTAL, KEY_VALUE_WIDTH), jnp.float32) ** block_levels(splits[11], (TENANT_TOTAL, KEY_VALUE_WIDTH), ((0, 4), (1, 4)), -0.2, 0.2)), 20.0, 600.0)
    return dict(activations=activations, output_gradient=output_gradient, row_tenant=row_tenant, group_row_count=group_row_count, tenant_storage_entry=tenant_storage_entry, key_value_weight=key_value_weight, adapter_down_maps=adapter_down_maps, adapter_up_maps=adapter_up_maps, down_row_factor=down_row_factor, down_column_factor=down_column_factor, up_row_factor=up_row_factor, up_column_factor=up_column_factor)


adapter_scale = 0.25
decay_rate = 0.9
tiny_floor = 1e-30

def slot_layout(tenant_col, tenant_storage_entry, row_limit):
    tenants = tenant_col[:, 0]
    count_rows = tenants.shape[0]
    entries = tenant_storage_entry.shape[0]
    onehot = (tenants[:, None] == jnp.arange(entries, dtype=jnp.int32)[None, :]).astype(jnp.int32)
    position = jnp.cumsum(onehot, axis=0) - onehot
    within = lax.optimization_barrier(jnp.sum(position * onehot, axis=1)).astype(jnp.int32)
    entry_of = lax.optimization_barrier(jnp.sum(onehot * tenant_storage_entry[None, :], axis=1)).astype(jnp.int32)
    target = (entry_of * row_limit + within).astype(jnp.int32)
    lookup = jnp.full((entries * row_limit,), count_rows, jnp.int32).at[target].set(jnp.arange(count_rows, dtype=jnp.int32))
    return (target, lookup)

def reference(activations, output_gradient, row_tenant, group_row_count, tenant_storage_entry, key_value_weight, adapter_down_maps, adapter_up_maps, down_row_factor, down_column_factor, up_row_factor, up_column_factor):
    live_mask = (jnp.arange(TOK, dtype=jnp.int32)[None, :] < group_row_count[:, None]).reshape(TOKENS, 1)
    masked = jnp.where(live_mask, output_gradient, jnp.zeros_like(output_gradient))
    frozen = jnp.dot(masked, key_value_weight.T, preferred_element_type=jnp.float32)
    target, lookup = jax.vmap(lambda column: slot_layout(column, tenant_storage_entry, TENANT_ROW_LIMIT))(row_tenant.reshape(N_DP, TOK, 1))
    padded_x = jnp.concatenate([activations.reshape(N_DP, TOK, MODEL_WIDTH), jnp.zeros((N_DP, 1, MODEL_WIDTH), activations.dtype)], axis=1)
    padded_g = jnp.concatenate([masked.reshape(N_DP, TOK, KEY_VALUE_WIDTH), jnp.zeros((N_DP, 1, KEY_VALUE_WIDTH), masked.dtype)], axis=1)
    group_numbers = jnp.arange(N_DP, dtype=jnp.int32)[:, None]

    def per_entry(written_rows, entry_number):
        storage_index = lax.dynamic_slice_in_dim(lookup, entry_number * TENANT_ROW_LIMIT, TENANT_ROW_LIMIT, 1)
        picked_input = padded_x[group_numbers, storage_index].reshape(N_DP * TENANT_ROW_LIMIT, MODEL_WIDTH)
        picked_gradient = padded_g[group_numbers, storage_index].reshape(N_DP * TENANT_ROW_LIMIT, KEY_VALUE_WIDTH)
        down_entry_map = adapter_down_maps[entry_number]
        up_entry_map = adapter_up_maps[entry_number]
        proj_down = jnp.dot(picked_input, down_entry_map, preferred_element_type=jnp.float32)
        proj_up = jnp.dot(picked_gradient, up_entry_map.T, preferred_element_type=jnp.float32)
        rounded_down = proj_down.astype(jnp.bfloat16)
        rounded_up = proj_up.astype(jnp.bfloat16)
        down_gradient = adapter_scale * jnp.dot(picked_input.T, rounded_up, preferred_element_type=jnp.float32)
        up_gradient = adapter_scale * jnp.dot(rounded_down.T, picked_gradient, preferred_element_type=jnp.float32)
        adapter_branch = (adapter_scale * jnp.dot(rounded_up, down_entry_map.T, preferred_element_type=jnp.float32)).astype(jnp.bfloat16)
        written_rows = written_rows.at[group_numbers, storage_index].set(adapter_branch.reshape(N_DP, TENANT_ROW_LIMIT, MODEL_WIDTH))
        return (written_rows, (down_gradient, up_gradient))
    blank_rows = jnp.zeros((N_DP, TOK + 1, MODEL_WIDTH), jnp.bfloat16)
    side_all, grads = lax.scan(per_entry, blank_rows, jnp.arange(TENANT_TOTAL, dtype=jnp.int32))
    down_gradient, up_gradient = grads
    side_rows = side_all[:, :TOK, :].reshape(TOKENS, MODEL_WIDTH)
    input_grad = (frozen + side_rows.astype(jnp.float32)).astype(jnp.bfloat16)
    square_down = down_gradient * down_gradient + tiny_floor
    square_up = up_gradient * up_gradient + tiny_floor
    down_rows = decay_rate * down_row_factor + (1.0 - decay_rate) * lax.optimization_barrier(jnp.mean(square_down, axis=2))
    down_cols = decay_rate * down_column_factor + (1.0 - decay_rate) * lax.optimization_barrier(jnp.mean(square_down, axis=1))
    up_rows = decay_rate * up_row_factor + (1.0 - decay_rate) * lax.optimization_barrier(jnp.mean(square_up, axis=2))
    up_cols = decay_rate * up_column_factor + (1.0 - decay_rate) * lax.optimization_barrier(jnp.mean(square_up, axis=1))
    second_down = down_rows[:, :, None] * down_cols[:, None, :] / lax.optimization_barrier(jnp.mean(down_rows, axis=1))[:, None, None]
    second_up = up_rows[:, :, None] * up_cols[:, None, :] / lax.optimization_barrier(jnp.mean(up_rows, axis=1))[:, None, None]
    down_update = down_gradient * lax.rsqrt(second_down)
    up_update = up_gradient * lax.rsqrt(second_up)
    return (input_grad, down_rows, down_cols, up_rows, up_cols, down_update, up_update)
```

```python
import jax
import jax.numpy as jnp
from jax import lax
from jax.experimental import pallas as pl
from jax.experimental.pallas import tpu as pltpu
from jax.sharding import PartitionSpec as P

adapter_scale = 0.25
decay_rate = 0.9
tiny_floor = 1e-30


def slot_layout(tenant_col, tenant_storage_entry, row_limit):
    tenants = tenant_col[:, 0]
    count_rows = tenants.shape[0]
    entries = tenant_storage_entry.shape[0]
    onehot = (tenants[:, None] == jnp.arange(entries, dtype=jnp.int32)[None, :]).astype(jnp.int32)
    position = jnp.cumsum(onehot, axis=0) - onehot
    within = jnp.sum(position * onehot, axis=1)
    entry_of = jnp.sum(onehot * tenant_storage_entry[None, :], axis=1)
    target = entry_of * row_limit + within
    lookup = (
        jnp.full((entries * row_limit,), count_rows, jnp.int32)
        .at[target]
        .set(jnp.arange(count_rows, dtype=jnp.int32))
    )
    return (target, lookup)


def native_shards(
    activations,
    output_gradient,
    row_tenant,
    group_row_count,
    tenant_storage_entry,
    key_value_weight,
    adapter_down_maps,
    adapter_up_maps,
    down_row_factor,
    down_column_factor,
    up_row_factor,
    up_column_factor,
):
    group_total = lax.axis_size("dp")
    owned_row_count = adapter_down_maps.shape[0]
    entries = owned_row_count * group_total
    count_rows = activations.shape[0]
    row_limit = 2 * count_rows // entries
    full_width = key_value_weight.shape[0] * lax.axis_size("tensor")
    pair_width = key_value_weight.shape[1]
    live_mask = jnp.arange(count_rows, dtype=jnp.int32)[:, None] < group_row_count[0]
    masked = jnp.where(live_mask, output_gradient, jnp.zeros_like(output_gradient))
    frozen = lax.dot_general(
        lax.all_gather(masked, "tensor", axis=1, tiled=True),
        key_value_weight,
        (((1,), (1,)), ((), ())),
        preferred_element_type=jnp.float32,
    )
    target, lookup = slot_layout(row_tenant, tenant_storage_entry, row_limit)
    padded_x = jnp.concatenate(
        [activations, jnp.zeros((1, activations.shape[1]), activations.dtype)], axis=0
    )
    padded_g = jnp.concatenate([masked, jnp.zeros((1, masked.shape[1]), masked.dtype)], axis=0)
    storage_input = padded_x[lookup]
    slot_g = padded_g[lookup]
    every_down, every_up = (
        lax.all_gather(adapter_down_maps, "dp", axis=0, tiled=True),
        lax.all_gather(adapter_up_maps, "dp", axis=0, tiled=True),
    )
    group_x = storage_input.reshape(entries, row_limit, storage_input.shape[1])
    group_g = slot_g.reshape(entries, row_limit, slot_g.shape[1])
    partial_down = jnp.einsum(
        "tcd,tdr->tcr", group_x, every_down, preferred_element_type=jnp.float32
    )
    partial_up = jnp.einsum("tck,trk->tcr", group_g, every_up, preferred_element_type=jnp.float32)
    proj_down, proj_up = lax.psum((partial_down, partial_up), "tensor")
    rounded_down = proj_down.astype(jnp.bfloat16)
    rounded_up = proj_up.astype(jnp.bfloat16)
    term_down = adapter_scale * jnp.einsum(
        "tcd,tcr->tdr", group_x, rounded_up, preferred_element_type=jnp.float32
    )
    term_up = adapter_scale * jnp.einsum(
        "tcr,tck->trk", rounded_down, group_g, preferred_element_type=jnp.float32
    )
    down_gradient, up_gradient = (
        lax.psum_scatter(term_down, "dp", scatter_dimension=0, tiled=True),
        lax.psum_scatter(term_up, "dp", scatter_dimension=0, tiled=True),
    )
    adapter_branch = (
        adapter_scale
        * jnp.einsum("tcr,tdr->tcd", rounded_up, every_down, preferred_element_type=jnp.float32)
    ).astype(jnp.bfloat16)
    side_slots = adapter_branch.reshape(entries * row_limit, storage_input.shape[1])
    side_rows = side_slots[target]
    input_grad = (frozen + side_rows.astype(jnp.float32)).astype(jnp.bfloat16)
    square_down = down_gradient * down_gradient + tiny_floor
    square_up = up_gradient * up_gradient + tiny_floor
    down_rows = decay_rate * down_row_factor + (1.0 - decay_rate) * jnp.mean(square_down, axis=2)
    up_cols = decay_rate * up_column_factor + (1.0 - decay_rate) * jnp.mean(square_up, axis=1)
    column_total, row_total, rows_sum = lax.psum(
        (jnp.sum(square_down, axis=1), jnp.sum(square_up, axis=2), jnp.sum(down_rows, axis=1)),
        "tensor",
    )
    down_cols = decay_rate * down_column_factor + (1.0 - decay_rate) * (column_total / full_width)
    up_rows = decay_rate * up_row_factor + (1.0 - decay_rate) * (row_total / pair_width)
    second_down = (
        down_rows[:, :, None] * down_cols[:, None, :] / (rows_sum / full_width)[:, None, None]
    )
    second_up = up_rows[:, :, None] * up_cols[:, None, :] / jnp.mean(up_rows, axis=1)[:, None, None]
    down_update = down_gradient * lax.rsqrt(second_down)
    up_update = up_gradient * lax.rsqrt(second_up)
    return (input_grad, down_rows, down_cols, up_rows, up_cols, down_update, up_update)


LANES = 128


def dot(a, b, ca, cb):
    return lax.dot_general(a, b, (((ca,), (cb,)), ((), ())), preferred_element_type=jnp.float32)


def fold_lanes(acc, rank):
    total = acc
    for shift in range(rank, LANES, rank):
        total = total + pltpu.roll(total if shift == rank else acc, shift, 1)
    return total


def project_body(rank, first, scal, x, g, e, *rest):
    maps, out = rest[:4], rest[-1]
    rows = x.shape[0]
    start = pl.program_id(0) * rows

    @pl.when(start < scal[2])
    def _():
        part = lax.broadcasted_iota(jnp.int32, (rows, LANES), 1) // rank
        row = start + lax.broadcasted_iota(jnp.int32, (rows, LANES), 0)
        sums = []
        for side, source in ((0, x), (1, g)):
            acc = jnp.zeros((rows, LANES), jnp.float32)
            for block in range(2):
                table = maps[2 * side + block]
                product = dot(source[...], table[...], 1, 1)
                for k in range(table.shape[0] // LANES):
                    hit = e[...] == scal[block] + k * (LANES // rank) + part
                    acc = acc + jnp.where(hit, product[:, k * LANES : (k + 1) * LANES], 0.0)
            sums.append(fold_lanes(acc, rank))
        total = jnp.where(part == 0, sums[0], sums[1])
        total = jnp.where(row < scal[2], total, 0.0)
        if not first:
            total = total + rest[4][...]
        out[...] = total

    @pl.when(start >= scal[2])
    def _():
        out[...] = jnp.zeros_like(out)


def project(scal, x, g, e, downs, ups, rank, blocks, prev=None):
    count_rows, width = x.shape
    rows = count_rows // blocks
    kv = g.shape[1]
    size = downs[0].shape[0]

    def by_row(i, s):
        return (i, 0)

    def whole(i, s):
        return (0, 0)

    specs = [
        pl.BlockSpec((rows, width), by_row),
        pl.BlockSpec((rows, kv), by_row),
        pl.BlockSpec((rows, LANES), by_row),
        pl.BlockSpec((size, width), whole),
        pl.BlockSpec((size, width), whole),
        pl.BlockSpec((size, kv), whole),
        pl.BlockSpec((size, kv), whole),
    ]
    args = [x, g, e, *downs, *ups]
    if prev is not None:
        specs.append(pl.BlockSpec((rows, LANES), by_row))
        args.append(prev)

    def kernel(*refs):
        project_body(rank, prev is None, *refs)

    return pl.pallas_call(
        kernel,
        grid_spec=pltpu.PrefetchScalarGridSpec(
            num_scalar_prefetch=1,
            grid=(blocks,),
            in_specs=specs,
            out_specs=pl.BlockSpec((rows, LANES), by_row),
        ),
        out_shape=jax.ShapeDtypeStruct((count_rows, LANES), jnp.float32),
        name="project",
    )(scal, *args)


def spread(value, e, base, size, rank):
    part = lax.broadcasted_iota(jnp.int32, value.shape, 1) // rank
    pieces = []
    for k in range(size // LANES):
        hit = e == base + k * (LANES // rank) + part
        pieces.append(jnp.where(hit, value, 0.0).astype(jnp.bfloat16))
    return pieces


def twice(both, rank):
    value = both.astype(jnp.float32)
    part = lax.broadcasted_iota(jnp.int32, value.shape, 1) // rank
    turned = pltpu.roll(value, rank, 1)
    return (jnp.where(part == 0, value, turned), jnp.where(part == 0, turned, value))


def gradients(scal, both, e, x, g, size, rank):
    count_rows, width = x.shape
    kv = g.shape[1]
    tiles = width // kv

    def kernel(scal, both, e, x, g, sent, kept, up_wide, down_wide):
        j = pl.program_id(0)

        @pl.when(j == 0)
        def _():
            d, u = twice(both[...], rank)
            for block in range(2):
                for wide, value in ((up_wide, u), (down_wide, d)):
                    for k, piece in enumerate(spread(value, e[...], scal[block], size, rank)):
                        at = block * size + k * LANES
                        wide[:, at : at + LANES] = piece

        def put(result):
            result = adapter_scale * result
            sent[...] = result[:size].astype(jnp.bfloat16)
            kept[...] = result[size:]

        @pl.when(j < tiles)
        def _():
            put(dot(up_wide[...], x[...], 0, 0))

        @pl.when(j == tiles)
        def _():
            put(dot(down_wide[...], g[...], 0, 0))

    return pl.pallas_call(
        kernel,
        grid_spec=pltpu.PrefetchScalarGridSpec(
            num_scalar_prefetch=1,
            grid=(tiles + 1,),
            in_specs=[
                pl.BlockSpec((count_rows, LANES), lambda j, s: (0, 0)),
                pl.BlockSpec((count_rows, LANES), lambda j, s: (0, 0)),
                pl.BlockSpec((count_rows, kv), lambda j, s: (0, jnp.minimum(j, tiles - 1))),
                pl.BlockSpec((count_rows, kv), lambda j, s: (0, 0)),
            ],
            out_specs=[
                pl.BlockSpec((size, kv), lambda j, s: (0, j)),
                pl.BlockSpec((size, kv), lambda j, s: (0, j)),
            ],
            scratch_shapes=[
                pltpu.VMEM((count_rows, 2 * size), jnp.bfloat16),
                pltpu.VMEM((count_rows, 2 * size), jnp.bfloat16),
            ],
        ),
        out_shape=[
            jax.ShapeDtypeStruct((size, width + kv), jnp.bfloat16),
            jax.ShapeDtypeStruct((size, width + kv), jnp.float32),
        ],
        name="gradients",
    )(scal, both, e, x, g)


def input_chunk(scal, chunk, chunks, g, near, both, e, weight, downs, out, rank):
    count_rows, kv = g.shape
    width = weight.shape[0]
    rows = count_rows // chunks
    size = downs[0].shape[0]
    tiles = width // kv

    def kernel(scal, own, left, right, far, wrap, both, e, w0, w1, w2, w3, *rest):
        maps, result, wide = rest[: len(downs)], rest[-2], rest[-1]
        j = pl.program_id(0)
        start = chunk * rows

        @pl.when((j == 0) & (start < scal[5]))
        def _():
            u = twice(both[...], rank)[1]
            for block in range(len(downs)):
                for k, piece in enumerate(spread(u, e[...], scal[6 + block], size, rank)):
                    at = block * size + k * LANES
                    wide[:, at : at + LANES] = piece

        @pl.when(start < scal[5])
        def _():
            from_left = jnp.where(scal[4] < 0, wrap[...], left[...])
            from_right = jnp.where(scal[4] > 0, wrap[...], right[...])
            acc = dot(own[...], w0[...], 1, 1)
            acc = acc + dot(from_left, w1[...], 1, 1)
            acc = acc + dot(from_right, w2[...], 1, 1)
            acc = acc + dot(far[...], w3[...], 1, 1)
            side = jnp.zeros_like(acc)
            for block, table in enumerate(maps):
                side = side + dot(wide[:, block * size : (block + 1) * size], table[...], 1, 0)
            side = (adapter_scale * side).astype(jnp.bfloat16).astype(jnp.float32)
            row = start + lax.broadcasted_iota(jnp.int32, acc.shape, 0)
            result[...] = jnp.where(row < scal[5], acc + side, 0.0).astype(jnp.bfloat16)

        @pl.when(start >= scal[5])
        def _():
            result[...] = jnp.zeros_like(result)

    def at_chunk(j, s):
        return (chunk, 0)

    def whole(j, s):
        return (0, 0)

    def weight_spec(slot):
        return pl.BlockSpec((kv, kv), lambda j, s: (j, s[slot]))

    specs = [pl.BlockSpec((rows, kv), at_chunk)]
    specs += [pl.BlockSpec((rows, kv), whole)] * 4
    specs += [pl.BlockSpec((rows, LANES), at_chunk)] * 2
    specs += [weight_spec(k) for k in range(4)]
    specs += [pl.BlockSpec((size, kv), lambda j, s: (0, j))] * len(downs)
    args = [scal, g, *near, both, e, weight, weight, weight, weight, *downs]
    aliases = {}
    if out is not None:
        specs.append(pl.BlockSpec(memory_space=pl.ANY))
        aliases = {len(args): 0}
        args.append(out)
    return pl.pallas_call(
        kernel,
        grid_spec=pltpu.PrefetchScalarGridSpec(
            num_scalar_prefetch=1,
            grid=(tiles,),
            in_specs=specs,
            out_specs=pl.BlockSpec((rows, kv), lambda j, s: (chunk, j)),
            scratch_shapes=[pltpu.VMEM((rows, len(downs) * size), jnp.bfloat16)],
        ),
        out_shape=jax.ShapeDtypeStruct((count_rows, width), jnp.bfloat16),
        input_output_aliases=aliases,
        name="input_chunk",
    )(*args)


def permute_shards(
    activations,
    output_gradient,
    row_tenant,
    group_row_count,
    tenant_storage_entry,
    key_value_weight,
    adapter_down_maps,
    adapter_up_maps,
    down_row_factor,
    down_column_factor,
    up_row_factor,
    up_column_factor,
):
    group_total = lax.axis_size("dp")
    line = lax.axis_size("tensor")
    here = lax.axis_index("tensor")
    group = lax.axis_index("dp")
    owned, width, rank = adapter_down_maps.shape
    kv = adapter_up_maps.shape[2]
    size = owned * rank
    count_rows = activations.shape[0]
    full_width = width * line
    pair_width = kv * line
    chunks = line
    rows = count_rows // chunks
    x, g = activations, output_gradient

    sibling = [(i, i ^ 1) for i in range(group_total)]
    across = [(i, i ^ 2) for i in range(group_total)]
    rightward = [(i, i + 1) for i in range(line - 1)]
    leftward = [(i + 1, i) for i in range(line - 1)]
    half = [(i, (i + line // 2) % line) for i in range(line)]
    ends = [(line - 2, line - 1), (1, 0)]

    def shift(value, step):
        perm = [(i, (i + step) % line) for i in range(line)]
        return lax.ppermute(value, "tensor", perm)

    own_down = jnp.swapaxes(adapter_down_maps, 1, 2).reshape(size, width)
    own_up = adapter_up_maps.reshape(size, kv)
    far_down = lax.ppermute(own_down, "dp", across)
    far_up = lax.ppermute(own_up, "dp", across)
    side_down = lax.ppermute(own_down, "dp", sibling)
    side_up = lax.ppermute(own_up, "dp", sibling)
    cross_down = lax.ppermute(far_down, "dp", sibling)
    cross_up = lax.ppermute(far_up, "dp", sibling)

    near = []
    for c in range(chunks):
        piece = g[c * rows : (c + 1) * rows]
        far = lax.ppermute(piece, "tensor", half)
        left = lax.ppermute(piece, "tensor", rightward)
        right = lax.ppermute(piece, "tensor", leftward)
        wrap = lax.ppermute(far, "tensor", ends)
        near.append((left, right, far, wrap))

    entry_count = tenant_storage_entry.shape[0]
    named = row_tenant == jnp.arange(entry_count, dtype=jnp.int32)[None, :]
    entry = jnp.sum(jnp.where(named, tenant_storage_entry[None, :], 0), axis=1, keepdims=True)
    e = jnp.broadcast_to(entry, (count_rows, LANES))
    count = group_row_count[0]
    base = [owned * group, owned * (group ^ 1), owned * (group ^ 2), owned * (group ^ 3)]

    def table(*values):
        return jnp.stack([jnp.asarray(v, jnp.int32) for v in values])

    partial = project(
        table(base[0], base[1], count), x, g, e, (own_down, side_down), (own_up, side_up), rank, chunks
    )
    partial = project(
        table(base[2], base[3], count),
        x,
        g,
        e,
        (far_down, cross_down),
        (far_up, cross_up),
        rank,
        chunks,
        partial,
    )

    def rows_of(index):
        return lax.dynamic_slice_in_dim(partial, index * rows, rows, 0)

    total = rows_of(here)
    for step in range(1, line):
        total = total + shift(rows_of((here + step) % line), step)
    rounded = total.astype(jnp.bfloat16)
    both = jnp.zeros((count_rows, LANES), jnp.bfloat16)
    for step in range(line):
        piece = shift(rounded, step) if step else rounded
        both = lax.dynamic_update_slice_in_dim(both, piece, (here - step) % line * rows, 0)

    sent, kept_far = gradients(table(base[3], base[2]), both, e, x, g, size, rank)
    got = lax.ppermute(sent, "dp", sibling)
    sent, kept = gradients(table(base[1], base[0]), both, e, x, g, size, rank)
    kept = kept + lax.ppermute(sent, "dp", sibling).astype(jnp.float32)
    outgoing = (kept_far + got.astype(jnp.float32)).astype(jnp.bfloat16)
    grad = kept + lax.ppermute(outgoing, "dp", across).astype(jnp.float32)

    down_gradient = grad[:, :width].reshape(owned, rank, width)
    up_gradient = grad[:, width:].reshape(owned, rank, kv)
    square_down = down_gradient * down_gradient + tiny_floor
    square_up = up_gradient * up_gradient + tiny_floor
    down_rows = decay_rate * down_row_factor + (1.0 - decay_rate) * jnp.mean(square_down, axis=1)
    up_cols = decay_rate * up_column_factor + (1.0 - decay_rate) * jnp.mean(square_up, axis=1)
    spill = jnp.zeros((owned, rank), jnp.float32)
    stats = jnp.concatenate(
        [
            jnp.concatenate([jnp.sum(square_down, axis=2), jnp.sum(square_up, axis=2)], axis=1),
            jnp.concatenate([spill + jnp.sum(down_rows, axis=1)[:, None], spill], axis=1),
        ],
        axis=0,
    )
    sums = stats
    for step in range(1, line):
        sums = sums + shift(stats, step)
    column_total, row_total = sums[:owned, :rank], sums[:owned, rank:]
    rows_sum = sums[owned:, :1]
    down_cols = decay_rate * down_column_factor + (1.0 - decay_rate) * (column_total / full_width)
    up_rows = decay_rate * up_row_factor + (1.0 - decay_rate) * (row_total / pair_width)
    second_down = (
        down_cols[:, :, None] * down_rows[:, None, :] / (rows_sum / full_width)[:, :, None]
    )
    second_up = up_rows[:, :, None] * up_cols[:, None, :] / jnp.mean(up_rows, axis=1)[:, None, None]
    down_update = jnp.swapaxes(down_gradient * lax.rsqrt(second_down), 1, 2)
    up_update = up_gradient * lax.rsqrt(second_up)

    wrapped = jnp.where(here == 0, -1, jnp.where(here == line - 1, 1, 0))
    scal = table(
        here,
        (here - 1) % line,
        (here + 1) % line,
        (here + 2) % line,
        wrapped,
        count,
        *base,
    )
    input_grad = None
    for c in range(chunks):
        maps = (own_down, side_down, far_down, cross_down)
        input_grad = input_chunk(
            scal, c, chunks, g, near[c], both, e, key_value_weight, maps, input_grad, rank
        )
    return (input_grad, down_rows, down_cols, up_rows, up_cols, down_update, up_update)


def staged(*args):
    return permute_shards(*args)


def solution(mesh):
    small = mesh.shape["tensor"] == 4 and mesh.shape["dp"] == 4
    body = staged if small else native_shards
    in_specs = (
        P(("rep", "dp"), "tensor"),
        P(("rep", "dp"), "tensor"),
        P(("rep", "dp"), None),
        P(("rep", "dp")),
        P(),
        P("tensor", None),
        P("dp", "tensor", None),
        P("dp", None, "tensor"),
        P("dp", "tensor"),
        P("dp", None),
        P("dp", None),
        P("dp", "tensor"),
    )
    out_specs = (
        P(("rep", "dp"), "tensor"),
        P(("rep", "dp"), "tensor"),
        P(("rep", "dp"), None),
        P(("rep", "dp"), None),
        P(("rep", "dp"), "tensor"),
        P(("rep", "dp"), "tensor", None),
        P(("rep", "dp"), None, "tensor"),
    )
    return jax.shard_map(body, mesh=mesh, in_specs=in_specs, out_specs=out_specs, check_vma=False)
```
